32 devices in a mesh: land: 2 (over x), dp: 16 (over z, y, core).
Axes of the slice: x: 2, y: 2, z: 4, core: 2. Of those that a mesh axis runs over, the one named last changes fastest.
Arguments:
- embeddings: bfloat16 [8192, 1280], P(('dp', 'land')), may hold values from -6 to 6
- landmarks: bfloat16 [2048, 1280], P(('land', 'dp')), may hold values from -6 to 6
- factor: bfloat16 [2048, 1024], P(('land', 'dp')), may hold values from -6 to 6
- centroids: bfloat16 [4096, 1024], P('land'), may hold values from -6 to 6
- assignment: int32 [8192], P('dp'), may hold values from 0 to 4095, as said below
Outputs:
- distances: float32 [8192, 4096], P('dp', 'land')
- new_centroids: float32 [4096, 1024], P(('land', 'dp'))
The draws below stay inside these ranges and needn't reach their ends.
Inputs may be any that keep to these rules, and one draw needn't show every extreme that they name: `assignment`: among the 512 rows of one index of dp, at most 32 are assigned to centroids of any one aligned block of 128 centroid numbers.
All inputs are finite; a program needn't handle non-finite values.
Results may differ from the reference program's by a relative error of at most 0.01.
Values may be sent and summed in bfloat16 or wider, within the bound.
No kernel may reach another device: no remote copies, remote signals or barrier semaphores. Data moves between devices by JAX's collectives and lax.ppermute only.
A program may use at most 64 MiB of HBM per device.

```python
import jax
import jax.numpy as jnp
from jax import lax

E = 1280
F = 1024
KC = 4096
ROWS = 512
LM_BLOCK = 1024
N_ROWS = 8192
LANDMARKS = 2048
OWN = 128
SLOTS = 32
N_LAND = 2
N_DP = 16


def centres_of(key):
    clusters = max(LANDMARKS // 32, 2)
    return jax.random.truncated_normal(jax.random.fold_in(key, 7), -4.0, 4.0, (clusters, E), jnp.float32)


def clustered(key, count, tag):
    centres = centres_of(key)
    own_key = jax.random.fold_in(key, tag)
    member = jax.random.randint(jax.random.fold_in(own_key, 1), (count,), 0, centres.shape[0])
    noise_part = jax.random.truncated_normal(jax.random.fold_in(own_key, 2), -4.0, 4.0, (count, E), jnp.float32)
    mix_weight = jax.random.uniform(jax.random.fold_in(own_key, 3), (count, 1), jnp.float32, 0.5, 0.95)
    points = mix_weight * centres[member] + jnp.sqrt(1.0 - mix_weight * mix_weight) * noise_part
    return jnp.clip(points, -6.0, 6.0)


def draw_embeddings(key, part):
    return clustered(key, N_ROWS, 11).astype(jnp.bfloat16)


def draw_landmarks(key, part):
    return clustered(key, LANDMARKS, 13).astype(jnp.bfloat16)


def draw_assignment(key, part):
    slices = N_LAND * N_DP
    seat_total = slices * SLOTS
    full_slice = jax.random.randint(jax.random.fold_in(key, 101), (), 0, slices)
    seat_ids = jnp.arange(seat_total, dtype=jnp.int32)

    def one_block(block_key):
        seat_order = jax.random.permutation(jax.random.fold_in(block_key, 1), seat_total).astype(jnp.int32)
        forced = seat_ids // SLOTS == full_slice
        scores = jnp.where(forced, -1 - seat_ids % SLOTS, seat_order)
        chosen = jnp.argsort(scores, stable=True)[:ROWS].astype(jnp.int32)
        shuffle = jax.random.permutation(jax.random.fold_in(block_key, 2), ROWS)
        chosen = chosen[shuffle]
        within = jax.random.randint(jax.random.fold_in(block_key, 3), (ROWS,), 0, OWN)
        return chosen // SLOTS * OWN + within
    block_keys = jax.random.split(jax.random.fold_in(key, 103), N_DP)
    return jax.vmap(one_block)(block_keys).reshape(N_ROWS).astype(jnp.int32)


def level_of(rng, shape, cuts, smallest, high):
    gain = 1.0
    for position, parts in cuts:
        draws = jax.random.uniform(jax.random.fold_in(jax.random.fold_in(rng, 6), position), (parts,), jnp.float32, smallest / len(cuts), high / len(cuts))
        gain = gain * jnp.repeat(jnp.exp(draws), shape[position] // parts).reshape((-1,) + (1,) * (len(shape) - 1 - position))
    return gain


def gaussian(stream_key, shape, scale, bound, cuts=(), kind=jnp.bfloat16):
    array = scale * jax.random.normal(stream_key, shape, jnp.float32)
    if cuts:
        array = array * level_of(stream_key, shape, cuts, -0.22, 0.18)
    return jnp.clip(array, -bound, bound).astype(kind)


def setup_inputs(seed: int = 0) -> dict:
    seeds = jax.random.split(jax.random.key(seed), 6)
    embeddings = draw_embeddings(jax.random.fold_in(seeds[5], 71), 0)
    landmarks = draw_landmarks(jax.random.fold_in(seeds[5], 71), 0)
    factor = gaussian(seeds[2], (LANDMARKS, F), 1.0, 6.0, ((0, 32),))
    centroids = gaussian(seeds[3], (KC, F), 1.0, 6.0, ((0, 2),))
    assignment = draw_assignment(jax.random.fold_in(seeds[5], 71), 0)
    return dict(embeddings=embeddings, landmarks=landmarks, factor=factor, centroids=centroids, assignment=assignment)


EPSILON = 1e-06
SHARPNESS = 6.0

def reference(embeddings, landmarks, factor, centroids, assignment):
    land_scale = lax.rsqrt(lax.optimization_barrier(jnp.mean(jnp.square(landmarks.astype(jnp.float32)), axis=1)) + EPSILON)
    cent_sq = lax.optimization_barrier(jnp.sum(jnp.square(centroids.astype(jnp.float32)), axis=1))
    factor_blocks = factor.reshape(N_LAND, LM_BLOCK, F).astype(jnp.float32)
    row_groups = embeddings.reshape(N_DP, ROWS, E)

    def one_group(group_rows):
        row_scale = lax.rsqrt(lax.optimization_barrier(jnp.mean(jnp.square(group_rows.astype(jnp.float32)), axis=1)) + EPSILON)
        inner_dots = jnp.dot(group_rows, landmarks.T, preferred_element_type=jnp.float32)
        similarity = inner_dots * row_scale[:, None] * land_scale[None, :] / E
        kernel = jnp.exp(SHARPNESS * (similarity - 1.0)).astype(jnp.bfloat16)
        kernel_wide = kernel.reshape(ROWS, N_LAND, LM_BLOCK).astype(jnp.float32)
        partial_value = jnp.einsum('rbm,bmf->brf', kernel_wide, factor_blocks).astype(jnp.bfloat16)
        features = lax.optimization_barrier(jnp.sum(partial_value.astype(jnp.float32), axis=0)).astype(jnp.bfloat16)
        feat_sq = lax.optimization_barrier(jnp.sum(jnp.square(features.astype(jnp.float32)), axis=1))
        cross_term = jnp.dot(features, centroids.T, preferred_element_type=jnp.float32)
        group_dist = (feat_sq[:, None] + cent_sq[None, :] - 2.0 * cross_term) / F
        return (group_dist, features)
    group_dist, all_features = lax.map(one_group, row_groups)
    distances = group_dist.reshape(N_ROWS, KC)
    all_features = all_features.reshape(N_ROWS, F).astype(jnp.float32)
    totals = jax.ops.segment_sum(all_features, assignment, num_segments=KC)
    counts = jax.ops.segment_sum(jnp.ones((N_ROWS,), jnp.float32), assignment, num_segments=KC)
    new_centroids = totals / jnp.maximum(counts, 1.0)[:, None]
    return (distances, new_centroids)
```

```python
import jax
import jax.numpy as jnp
from jax import lax
from jax.sharding import PartitionSpec as P

EPSILON = 1e-06
SHARPNESS = 6.0


def split_dp(count):
    cores = 2 if count % 2 == 0 else 1
    outer = 4 if (count // cores) % 4 == 0 else 1
    return outer, count // cores // outer, cores


def shift_perm(sizes, axis, step):
    outer, middle, cores = sizes
    pairs = []
    for z in range(outer):
        for y in range(middle):
            for c in range(cores):
                target = [z, y, c]
                target[axis] = (target[axis] + step) % sizes[axis]
                pairs.append(((z * middle + y) * cores + c, (target[0] * middle + target[1]) * cores + target[2]))
    return pairs


def local(embeddings, landmarks, factor, centroids, assignment):
    land_count = lax.axis_size("land")
    dp_count = lax.axis_size("dp")
    land_id = lax.axis_index("land")
    sizes = split_dp(dp_count)
    own_rows, embed_width = embeddings.shape
    feat_width = factor.shape[1]
    group_rows = own_rows * land_count

    def move(x, axis, step):
        return lax.ppermute(x, "dp", shift_perm(sizes, axis, step))

    def gather(x):
        pieces = [x] + [move(x, 0, k) for k in range(1, sizes[0])]
        return pieces + [move(p, 1, k) for p in pieces for k in range(1, sizes[1])]

    def land_shift(x, step):
        return lax.ppermute(x, "land", [((s + step) % land_count, s) for s in range(land_count)])

    rows = jnp.zeros((group_rows, embed_width), embeddings.dtype)
    rows = lax.dynamic_update_slice(rows, embeddings, (land_id * own_rows, 0))
    for step in range(1, land_count):
        source = (land_id + step) % land_count
        rows = lax.dynamic_update_slice(rows, land_shift(embeddings, step), (source * own_rows, 0))
    groups = [rows] + [move(rows, 2, k) for k in range(1, sizes[2])]
    marks = jnp.concatenate(gather(landmarks), axis=0)
    factors = jnp.concatenate(gather(factor), axis=0)

    mark_scale = lax.rsqrt(jnp.mean(jnp.square(marks.astype(jnp.float32)), axis=1) + EPSILON)

    def partial_of(block):
        scale = lax.rsqrt(jnp.mean(jnp.square(block.astype(jnp.float32)), axis=1) + EPSILON) / embed_width
        dots = lax.dot_general(block, marks, (((1,), (1,)), ((), ())), preferred_element_type=jnp.float32)
        similarity = dots * scale[:, None] * mark_scale[None, :]
        kernel = jnp.exp(SHARPNESS * (similarity - 1.0)).astype(jnp.bfloat16)
        return jnp.dot(kernel, factors, preferred_element_type=jnp.float32)

    partial_value = partial_of(groups[0])
    for k in range(1, sizes[2]):
        other = partial_of(groups[k]).astype(jnp.bfloat16)
        partial_value = partial_value + move(other, 2, sizes[2] - k).astype(jnp.float32)
    partial_value = partial_value.astype(jnp.bfloat16)
    total = partial_value.astype(jnp.float32)
    for step in range(1, land_count):
        total = total + land_shift(partial_value, step).astype(jnp.float32)
    features = total.astype(jnp.bfloat16)

    feat_sq = jnp.sum(jnp.square(features.astype(jnp.float32)), axis=1)
    cent_sq = jnp.sum(jnp.square(centroids.astype(jnp.float32)), axis=1)
    cross_term = lax.dot_general(
        features, centroids, (((1,), (1,)), ((), ())), preferred_element_type=jnp.float32
    )
    distances = (feat_sq[:, None] + cent_sq[None, :] - 2.0 * cross_term) / feat_width
    cent_block = centroids.shape[0]
    own_width = cent_block // dp_count
    slot_count = 2 * max(1, group_rows // (land_count * dp_count))
    slice_id = assignment // own_width
    target_land = slice_id // dp_count
    target_dp = slice_id % dp_count
    local_id = assignment % own_width
    in_block = target_land == land_id
    row_pos = lax.iota(jnp.int32, group_rows)
    earlier = (
        (target_dp[None, :] == target_dp[:, None])
        & in_block[None, :]
        & (row_pos[None, :] < row_pos[:, None])
    )
    slot_rank = jnp.sum(earlier.astype(jnp.int32), axis=1)
    slot_of = jnp.where(in_block, target_dp * slot_count + slot_rank, -1)
    slot_pos = lax.iota(jnp.int32, dp_count * slot_count)
    slot_pick = slot_pos[:, None] == slot_of[None, :]
    slot_ids = jnp.max(jnp.where(slot_pick, local_id[None, :], -1), axis=1)
    slot_ids = slot_ids.reshape(dp_count, slot_count)
    arrived_ids = lax.all_to_all(slot_ids, "dp", split_axis=0, concat_axis=0, tiled=True)
    outgoing = jnp.dot(
        slot_pick.astype(jnp.bfloat16), features, preferred_element_type=jnp.float32
    ).astype(jnp.bfloat16)
    outgoing = outgoing.reshape(dp_count, slot_count, feat_width)
    arrived = lax.all_to_all(outgoing, "dp", split_axis=0, concat_axis=0, tiled=True)
    arrived = arrived.reshape(dp_count * slot_count, feat_width)
    arrived_ids = arrived_ids.reshape(dp_count * slot_count)
    id_match = arrived_ids[None, :] == lax.iota(jnp.int32, own_width)[:, None]
    cent_sums = jnp.dot(id_match.astype(jnp.bfloat16), arrived, preferred_element_type=jnp.float32)
    cent_counts = jnp.sum(id_match.astype(jnp.float32), axis=1)
    new_centroids = cent_sums / jnp.maximum(cent_counts, 1.0)[:, None]
    return (distances, new_centroids)


def solution(mesh):
    return jax.shard_map(
        local,
        mesh=mesh,
        in_specs=(
            P(("dp", "land"), None),
            P(("land", "dp"), None),
            P(("land", "dp"), None),
            P("land", None),
            P("dp"),
        ),
        out_specs=(P("dp", "land"), P(("land", "dp"), None)),
        check_vma=False,
    )
```

```python
import functools

import jax
import jax.numpy as jnp
from jax import lax
from jax.experimental import pallas as pl
from jax.experimental.pallas import tpu as pltpu
from jax.sharding import PartitionSpec as P


EPSILON = 1e-06
SHARPNESS = 6.0
FACTOR_PARTS = 2
VMEM = pl.BlockSpec(memory_space=pltpu.VMEM)
SMEM = pl.BlockSpec(memory_space=pltpu.SMEM)


def split_dp(count):
    cores = 2 if count % 2 == 0 else 1
    outer = 4 if (count // cores) % 4 == 0 else 1
    return outer, count // cores // outer, cores


def partner(index, size, step):
    return index ^ step if size & (size - 1) == 0 else (index + step) % size


def axis_perm(sizes, axis, step):
    outer, middle, cores = sizes
    pairs = []
    for z in range(outer):
        for y in range(middle):
            for c in range(cores):
                target = [z, y, c]
                target[axis] = partner(target[axis], sizes[axis], step)
                pairs.append(((z * middle + y) * cores + c, (target[0] * middle + target[1]) * cores + target[2]))
    return pairs


def call(body, outs, args, land, scratch=(), flops=0, limit=24):
    moved = sum(a.size * a.dtype.itemsize for a in list(args) + list(outs))
    return pl.pallas_call(
        body,
        out_shape=list(outs),
        in_specs=[SMEM] + [VMEM] * len(args),
        out_specs=[VMEM] * len(outs),
        scratch_shapes=[pltpu.VMEM(*s) for s in scratch],
        cost_estimate=pl.CostEstimate(flops=flops, bytes_accessed=moved, transcendentals=0),
        compiler_params=pltpu.CompilerParams(vmem_limit_bytes=limit * 2**20),
    )(land, *args)


def column_to_row(column):
    wide = jnp.broadcast_to(column, (column.shape[0], 128))
    return jnp.transpose(wide)[0:1]


def kernel_body(land_count, cores, pieces, land_ref, *refs):
    count = land_count * cores
    row_refs, mark_refs = refs[:count], refs[count : count + pieces]
    out_ref, marks = refs[count + pieces :]
    depth, width = mark_refs[0].shape
    rows = row_refs[0].shape[0]
    for i, piece in enumerate(mark_refs):
        marks[i * depth : (i + 1) * depth] = piece[...]
    square = jnp.square(marks[...].astype(jnp.float32))
    mark_scale = column_to_row(lax.rsqrt(jnp.sum(square, axis=1, keepdims=True) / width + EPSILON))
    for g in range(cores):
        for s in range(land_count):
            source = lax.rem(land_ref[0] + s, land_count)
            values = row_refs[g * land_count + s][...]
            square = jnp.square(values.astype(jnp.float32))
            scale = lax.rsqrt(jnp.sum(square, axis=1, keepdims=True) / width + EPSILON) / width
            dots = lax.dot_general(values, marks[...], (((1,), (1,)), ((), ())), preferred_element_type=jnp.float32)
            similarity = dots * scale * mark_scale
            offset = pl.multiple_of(g * land_count * rows + source * rows, rows)
            out_ref[pl.ds(offset, rows), :] = jnp.exp(SHARPNESS * (similarity - 1.0)).astype(out_ref.dtype)


def partial_body(land_count, cores, pieces, part, land_ref, kern_ref, *refs):
    piece_refs, (own_ref, *others, block) = refs[:pieces], refs[pieces:]
    depth, full = piece_refs[0].shape
    keep_width = full // land_count
    width = block.shape[1]
    rows = own_ref.shape[0]
    for s in range(land_count):
        source = lax.rem(land_ref[0] + s, land_count)
        columns = pl.ds(pl.multiple_of(source * keep_width + part * width, 128), width)
        for i, piece in enumerate(piece_refs):
            block[i * depth : (i + 1) * depth] = piece[:, columns]
        for g in reversed(range(cores)):
            out = own_ref if g == 0 else others[g - 1]
            value = jnp.dot(kern_ref[g * rows : (g + 1) * rows], block[...], preferred_element_type=jnp.float32)
            out[:, s * width : (s + 1) * width] = value.astype(out.dtype)


def add_body(count, land_ref, *refs):
    ins, outs = refs[:count], refs[count:]
    width = outs[0].shape[1]
    for s, out in enumerate(outs):
        total = ins[0][:, s * width : (s + 1) * width]
        for part in ins[1:]:
            total = total + part[:, s * width : (s + 1) * width].astype(jnp.float32)
        out[...] = total.astype(out.dtype)


def pick_body(count, land_ref, *refs):
    *ins, pick_ref, feat_ref, out_ref = refs
    total = ins[0][...].astype(jnp.float32)
    for part in ins[1:count]:
        total = total + part[...].astype(jnp.float32)
    features = total.astype(feat_ref.dtype)
    feat_ref[...] = features
    start = 0
    for done in ins[count:]:
        start = done.shape[1]
        out_ref[:, :start] = done[...]
    value = jnp.dot(pick_ref[...], features, preferred_element_type=jnp.float32)
    out_ref[:, start:] = value.astype(out_ref.dtype)


def distance_body(land_count, parts, land_ref, *refs):
    count = land_count * parts
    feats, cent_ref, out_ref, feat_sq = refs[:count], refs[count], refs[count + 1], refs[count + 2]

    @pl.when(pl.program_id(0) == 0)
    def _():
        total = jnp.zeros(feat_sq.shape, jnp.float32)
        for feat in feats:
            total = total + jnp.sum(jnp.square(feat[...].astype(jnp.float32)), axis=1, keepdims=True)
        feat_sq[...] = total

    cent = cent_ref[...]
    cent_sq = column_to_row(jnp.sum(jnp.square(cent.astype(jnp.float32)), axis=1, keepdims=True))
    width = feats[0].shape[1]
    cross = None
    for s in range(land_count):
        source = lax.rem(land_ref[0] + s, land_count)
        for h in range(parts):
            columns = pl.ds(pl.multiple_of((source * parts + h) * width, 128), width)
            term = lax.dot_general(
                feats[s * parts + h][...],
                cent_ref[:, columns],
                (((1,), (1,)), ((), ())),
                preferred_element_type=jnp.float32,
            )
            cross = term if cross is None else cross + term
    out_ref[...] = (feat_sq[...] + cent_sq - 2.0 * cross) / cent_ref.shape[1]


def mean_body(land_count, land_ref, ids_ref, arrived_ref, out_ref):
    own_width, width = out_ref.shape[0], arrived_ref.shape[1]
    slots = ids_ref.shape[1] // land_count
    for j in range(land_count):
        match = ids_ref[:, j * slots : (j + 1) * slots] == lax.broadcasted_iota(jnp.int32, (own_width, slots), 0)
        match = match.astype(jnp.float32)
        counts = jnp.sum(match, axis=1, keepdims=True)
        part = arrived_ref[j * slots : (j + 1) * slots]
        sums = jnp.dot(match.astype(jnp.bfloat16), part, preferred_element_type=jnp.float32)
        out_ref[:, j * width : (j + 1) * width] = sums / jnp.maximum(counts, 1.0)


def factor_parts(feat_width, land_count):
    return FACTOR_PARTS if feat_width % (128 * land_count * FACTOR_PARTS) == 0 else 1


def local(embeddings, landmarks, factor, centroids, assignment):
    land_count = lax.axis_size("land")
    dp_count = lax.axis_size("dp")
    land_id = lax.axis_index("land")
    land = land_id.astype(jnp.int32).reshape(1)
    sizes = split_dp(dp_count)
    cores = sizes[2]
    own_rows, embed_width = embeddings.shape
    feat_width = factor.shape[1]
    group_rows = own_rows * land_count
    bf16, f32 = jnp.bfloat16, jnp.float32

    def shape(rows, columns, dtype):
        return jax.ShapeDtypeStruct((rows, columns), dtype)

    def move(x, axis, step):
        return lax.ppermute(x, "dp", axis_perm(sizes, axis, step))

    def land_send(x, step):
        return lax.ppermute(x, "land", [(s, (s + step) % land_count) for s in range(land_count)])

    def outer_shifts(x):
        return [x] + [move(x, 0, k) for k in range(1, sizes[0])]

    def middle_shifts(pieces):
        return pieces + [move(p, 1, k) for p in pieces for k in range(1, sizes[1])]

    row_pieces = [embeddings] + [land_send(embeddings, land_count - k) for k in range(1, land_count)]
    row_pieces = row_pieces + [move(p, 2, k) for k in range(1, cores) for p in row_pieces]
    marks = middle_shifts(outer_shifts(landmarks))
    parts = factor_parts(feat_width, land_count)
    keep_width = feat_width // land_count
    width = keep_width // parts
    factors = middle_shifts(outer_shifts(factor))

    rows_all = group_rows * cores
    depth_all = landmarks.shape[0] * len(marks)
    (kern,) = call(
        functools.partial(kernel_body, land_count, cores, len(marks)),
        [shape(rows_all, depth_all, bf16)],
        row_pieces + marks,
        land,
        scratch=[((depth_all, embed_width), bf16)],
        flops=2 * rows_all * depth_all * embed_width,
    )
    keeps, sends = [], []
    for h in range(parts):
        own, *others = call(
            functools.partial(partial_body, land_count, cores, len(marks), h),
            [shape(group_rows, land_count * width, f32)]
            + [shape(group_rows, land_count * width, bf16)] * (cores - 1),
            [kern] + factors,
            land,
            scratch=[((depth_all, width), bf16)],
            flops=2 * rows_all * depth_all * land_count * width,
        )
        others = [move(o, 2, cores - g) for g, o in enumerate(others, 1)]
        keep, *send = call(
            functools.partial(add_body, cores), [shape(group_rows, width, bf16)] * land_count, [own] + others, land
        )
        keeps.append(keep)
        sends.append([land_send(x, s) for s, x in enumerate(send, 1)])

    own_width = centroids.shape[0] // dp_count
    slot_count = 2 * max(1, group_rows // (land_count * dp_count))
    slot_total = land_count * dp_count * slot_count
    everyone = ("land", "dp")
    slice_id = assignment // own_width
    local_id = assignment % own_width
    row_pos = lax.iota(jnp.int32, group_rows)
    earlier = (slice_id[None, :] == slice_id[:, None]) & (row_pos[None, :] < row_pos[:, None])
    slot_rank = jnp.sum(earlier.astype(jnp.int32), axis=1)
    slot_of = slice_id * slot_count + slot_rank
    slot_match = lax.iota(jnp.int32, slot_total)[:, None] == slot_of[None, :]
    slot_ids = jnp.max(jnp.where(slot_match, local_id[None, :], -1), axis=1)
    slot_pick = slot_match.astype(bf16)
    arrived_ids = lax.all_to_all(
        slot_ids.reshape(land_count * dp_count, slot_count), everyone, split_axis=0, concat_axis=0, tiled=True
    )
    arrived_ids = arrived_ids.reshape(1, slot_total)

    mine, outgoing = [], None
    for h in range(parts):
        before = [outgoing] if h else []
        feat, outgoing = call(
            functools.partial(pick_body, land_count),
            [shape(group_rows, width, bf16), shape(slot_total, (h + 1) * width, bf16)],
            [keeps[h]] + sends[h] + before + [slot_pick],
            land,
            flops=2 * group_rows * slot_total * width,
        )
        mine.append(feat)
    arrived = lax.all_to_all(
        outgoing.reshape(land_count * dp_count, slot_count, keep_width),
        everyone,
        split_axis=0,
        concat_axis=0,
        tiled=True,
    )
    arrived = arrived.reshape(slot_total, keep_width)
    feats = mine + [land_send(mine[h], land_count - s) for s in range(1, land_count) for h in range(parts)]

    cent_block = centroids.shape[0]
    block = min(256, cent_block)
    distances = pl.pallas_call(
        functools.partial(distance_body, land_count, parts),
        grid=(cent_block // block,),
        out_shape=shape(group_rows, cent_block, f32),
        in_specs=[SMEM]
        + [pl.BlockSpec((group_rows, width), lambda i: (0, 0))] * len(feats)
        + [pl.BlockSpec((block, feat_width), lambda i: (i, 0))],
        out_specs=pl.BlockSpec((group_rows, block), lambda i: (0, i)),
        scratch_shapes=[pltpu.VMEM((group_rows, 1), f32)],
        cost_estimate=pl.CostEstimate(
            flops=2 * group_rows * cent_block * feat_width,
            bytes_accessed=2 * cent_block * feat_width + 4 * group_rows * cent_block,
            transcendentals=0,
        ),
        compiler_params=pltpu.CompilerParams(vmem_limit_bytes=24 * 2**20),
        name="distances",
    )(land, *feats, centroids)
    (new_centroids,) = call(
        functools.partial(mean_body, land_count),
        [shape(own_width, feat_width, f32)],
        [arrived_ids, arrived],
        land,
        flops=2 * own_width * slot_total * keep_width,
    )
    return (distances, new_centroids)


def solution(mesh):
    return jax.shard_map(
        local,
        mesh=mesh,
        in_specs=(
            P(("dp", "land"), None),
            P(("land", "dp"), None),
            P(("land", "dp"), None),
            P("land", None),
            P("dp"),
        ),
        out_specs=(P("dp", "land"), P(("land", "dp"), None)),
        check_vma=False,
    )
```

```python
import functools

import jax
import jax.numpy as jnp
from jax import lax
from jax.experimental import pallas as pl
from jax.experimental.pallas import tpu as pltpu
from jax.sharding import PartitionSpec as P


EPSILON = 1e-06
SHARPNESS = 6.0
FACTOR_PARTS = 2
VMEM = pl.BlockSpec(memory_space=pltpu.VMEM)
SMEM = pl.BlockSpec(memory_space=pltpu.SMEM)


def split_dp(count):
    cores = 2 if count % 2 == 0 else 1
    outer = 4 if (count // cores) % 4 == 0 else 1
    return outer, count // cores // outer, cores


def partner(index, size, step):
    return index ^ step if size & (size - 1) == 0 else (index + step) % size


def axis_perm(sizes, axis, step):
    outer, middle, cores = sizes
    pairs = []
    for z in range(outer):
        for y in range(middle):
            for c in range(cores):
                target = [z, y, c]
                target[axis] = partner(target[axis], sizes[axis], step)
                pairs.append(((z * middle + y) * cores + c, (target[0] * middle + target[1]) * cores + target[2]))
    return pairs


def call(body, outs, args, land, scratch=(), flops=0, limit=24):
    moved = sum(a.size * a.dtype.itemsize for a in list(args) + list(outs))
    return pl.pallas_call(
        body,
        out_shape=list(outs),
        in_specs=[SMEM] + [VMEM] * len(args),
        out_specs=[VMEM] * len(outs),
        scratch_shapes=[pltpu.VMEM(*s) for s in scratch],
        cost_estimate=pl.CostEstimate(flops=flops, bytes_accessed=moved, transcendentals=0),
        compiler_params=pltpu.CompilerParams(vmem_limit_bytes=limit * 2**20),
    )(land, *args)


def column_to_row(column):
    wide = jnp.broadcast_to(column, (column.shape[0], 128))
    return jnp.transpose(wide)[0:1]


def stage_body(land_ref, *refs):
    for src, out in zip(refs[: len(refs) // 2], refs[len(refs) // 2 :]):
        out[...] = src[...]


def kernel_body(land_count, cores, pieces, land_ref, *refs):
    count = land_count * cores
    row_refs, mark_refs = refs[:count], refs[count : count + pieces]
    out_ref, marks = refs[count + pieces :]
    depth, width = mark_refs[0].shape
    rows = row_refs[0].shape[0]
    for i, piece in enumerate(mark_refs):
        marks[i * depth : (i + 1) * depth] = piece[...]
    square = jnp.square(marks[...].astype(jnp.float32))
    mark_scale = column_to_row(lax.rsqrt(jnp.sum(square, axis=1, keepdims=True) / width + EPSILON))
    for g in range(cores):
        for s in range(land_count):
            source = lax.rem(land_ref[0] + s, land_count)
            values = row_refs[g * land_count + s][...]
            square = jnp.square(values.astype(jnp.float32))
            scale = lax.rsqrt(jnp.sum(square, axis=1, keepdims=True) / width + EPSILON) / width
            dots = lax.dot_general(values, marks[...], (((1,), (1,)), ((), ())), preferred_element_type=jnp.float32)
            similarity = dots * scale * mark_scale
            offset = pl.multiple_of(g * land_count * rows + source * rows, rows)
            out_ref[pl.ds(offset, rows), :] = jnp.exp(SHARPNESS * (similarity - 1.0)).astype(out_ref.dtype)


def partial_body(land_count, cores, pieces, part, land_ref, kern_ref, *refs):
    piece_refs, (own_ref, *others, block) = refs[:pieces], refs[pieces:]
    depth, full = piece_refs[0].shape
    keep_width = full // land_count
    width = block.shape[1]
    rows = own_ref.shape[0]
    for s in range(land_count):
        source = lax.rem(land_ref[0] + s, land_count)
        columns = pl.ds(pl.multiple_of(source * keep_width + part * width, 128), width)
        for i, piece in enumerate(piece_refs):
            block[i * depth : (i + 1) * depth] = piece[:, columns]
        for g in reversed(range(cores)):
            out = own_ref if g == 0 else others[g - 1]
            value = jnp.dot(kern_ref[g * rows : (g + 1) * rows], block[...], preferred_element_type=jnp.float32)
            out[:, s * width : (s + 1) * width] = value.astype(out.dtype)


def add_body(count, land_ref, *refs):
    ins, outs = refs[:count], refs[count:]
    width = outs[0].shape[1]
    for s, out in enumerate(outs):
        total = ins[0][:, s * width : (s + 1) * width]
        for part in ins[1:]:
            total = total + part[:, s * width : (s + 1) * width].astype(jnp.float32)
        out[...] = total.astype(out.dtype)


def pick_body(count, land_ref, *refs):
    *ins, pick_ref, feat_ref, out_ref = refs
    total = ins[0][...].astype(jnp.float32)
    for part in ins[1:count]:
        total = total + part[...].astype(jnp.float32)
    features = total.astype(feat_ref.dtype)
    feat_ref[...] = features
    start = 0
    for done in ins[count:]:
        start = done.shape[1]
        out_ref[:, :start] = done[...]
    value = jnp.dot(pick_ref[...], features, preferred_element_type=jnp.float32)
    out_ref[:, start:] = value.astype(out_ref.dtype)


def square_sum(parts):
    total = None
    for part in parts:
        term = jnp.sum(jnp.square(part[...].astype(jnp.float32)), axis=1, keepdims=True)
        total = term if total is None else total + term
    return total


def cross_sum(feats, cent_ref, first, land_count, parts, land_ref):
    width = feats[0].shape[1]
    cross = None
    for i, feat in enumerate(feats):
        source = lax.rem(land_ref[0] + first + i // parts, land_count)
        columns = pl.ds(pl.multiple_of((source * parts + i % parts) * width, 128), width)
        term = lax.dot_general(
            feat[...], cent_ref[:, columns], (((1,), (1,)), ((), ())), preferred_element_type=jnp.float32
        )
        cross = term if cross is None else cross + term
    return cross


def near_body(land_count, parts, land_ref, *refs):
    *feats, cent_ref, out_ref, feat_sq = refs

    @pl.when(pl.program_id(0) == 0)
    def _():
        feat_sq[...] = square_sum(feats)

    cent_sq = column_to_row(jnp.sum(jnp.square(cent_ref[...].astype(jnp.float32)), axis=1, keepdims=True))
    cross = cross_sum(feats, cent_ref, 0, land_count, parts, land_ref)
    out_ref[...] = feat_sq[...] + cent_sq - 2.0 * cross


def distance_body(land_count, parts, land_ref, *refs):
    *feats, cent_ref, near_ref, out_ref, feat_sq = refs

    @pl.when(pl.program_id(0) == 0)
    def _():
        feat_sq[...] = square_sum(feats)

    cross = cross_sum(feats, cent_ref, 1, land_count, parts, land_ref)
    out_ref[...] = (near_ref[...] + feat_sq[...] - 2.0 * cross) / cent_ref.shape[1]


def mean_body(land_count, land_ref, ids_ref, arrived_ref, out_ref):
    own_width, width = out_ref.shape[0], arrived_ref.shape[1]
    slots = ids_ref.shape[1] // land_count
    for j in range(land_count):
        match = ids_ref[:, j * slots : (j + 1) * slots] == lax.broadcasted_iota(jnp.int32, (own_width, slots), 0)
        match = match.astype(jnp.float32)
        counts = jnp.sum(match, axis=1, keepdims=True)
        part = arrived_ref[j * slots : (j + 1) * slots]
        sums = jnp.dot(match.astype(jnp.bfloat16), part, preferred_element_type=jnp.float32)
        out_ref[:, j * width : (j + 1) * width] = sums / jnp.maximum(counts, 1.0)


def factor_parts(feat_width, land_count):
    return FACTOR_PARTS if feat_width % (128 * land_count * FACTOR_PARTS) == 0 else 1


def local(embeddings, landmarks, factor, centroids, assignment):
    land_count = lax.axis_size("land")
    dp_count = lax.axis_size("dp")
    land_id = lax.axis_index("land")
    land = land_id.astype(jnp.int32).reshape(1)
    sizes = split_dp(dp_count)
    cores = sizes[2]
    own_rows, embed_width = embeddings.shape
    feat_width = factor.shape[1]
    group_rows = own_rows * land_count
    bf16, f32 = jnp.bfloat16, jnp.float32

    def shape(rows, columns, dtype):
        return jax.ShapeDtypeStruct((rows, columns), dtype)

    def move(x, axis, step):
        return lax.ppermute(x, "dp", axis_perm(sizes, axis, step))

    def land_send(x, step):
        return lax.ppermute(x, "land", [(s, (s + step) % land_count) for s in range(land_count)])

    def along_z(x):
        pieces = [x]
        for k in range(1, sizes[0]):
            relayed = sizes[0] == 4 and k == 3
            pieces.append(move(pieces[2] if relayed else x, 0, 1 if relayed else k))
        return pieces

    def along_y(pieces, relay):
        out = list(pieces)
        for k in range(1, sizes[1]):
            first = move(pieces[0], 1, k)
            for i, piece in enumerate(pieces):
                if i == 0:
                    out.append(first)
                elif i == 1 and relay:
                    out.append(move(first, 0, 1))
                else:
                    out.append(move(piece, 1, k))
        return out

    row_pieces = [embeddings] + [land_send(embeddings, land_count - k) for k in range(1, land_count)]
    row_pieces = row_pieces + [move(p, 2, k) for k in range(1, cores) for p in row_pieces]
    marks = along_y(along_z(landmarks), False)
    parts = factor_parts(feat_width, land_count)
    keep_width = feat_width // land_count
    width = keep_width // parts
    factors = along_y(along_z(factor), sizes[0] > 1)

    rows_all = group_rows * cores
    depth_all = landmarks.shape[0] * len(marks)
    row_pieces[0], marks[0], factors[0] = call(
        stage_body,
        [shape(*a.shape, a.dtype) for a in (embeddings, landmarks, factor)],
        [embeddings, landmarks, factor],
        land,
    )
    (kern,) = call(
        functools.partial(kernel_body, land_count, cores, len(marks)),
        [shape(rows_all, depth_all, bf16)],
        row_pieces + marks,
        land,
        scratch=[((depth_all, embed_width), bf16)],
        flops=2 * rows_all * depth_all * embed_width,
    )
    keeps, sends = [], []
    for h in range(parts):
        own, *others = call(
            functools.partial(partial_body, land_count, cores, len(marks), h),
            [shape(group_rows, land_count * width, f32)]
            + [shape(group_rows, land_count * width, bf16)] * (cores - 1),
            [kern] + factors,
            land,
            scratch=[((depth_all, width), bf16)],
            flops=2 * rows_all * depth_all * land_count * width,
        )
        others = [move(o, 2, cores - g) for g, o in enumerate(others, 1)]
        keep, *send = call(
            functools.partial(add_body, cores), [shape(group_rows, width, bf16)] * land_count, [own] + others, land
        )
        keeps.append(keep)
        sends.append([land_send(x, s) for s, x in enumerate(send, 1)])

    own_width = centroids.shape[0] // dp_count
    slot_count = 2 * max(1, group_rows // (land_count * dp_count))
    slot_total = land_count * dp_count * slot_count
    everyone = ("land", "dp")
    slice_id = assignment // own_width
    local_id = assignment % own_width
    row_pos = lax.iota(jnp.int32, group_rows)
    earlier = (slice_id[None, :] == slice_id[:, None]) & (row_pos[None, :] < row_pos[:, None])
    slot_rank = jnp.sum(earlier.astype(jnp.int32), axis=1)
    slot_of = slice_id * slot_count + slot_rank
    slot_match = lax.iota(jnp.int32, slot_total)[:, None] == slot_of[None, :]
    slot_ids = jnp.max(jnp.where(slot_match, local_id[None, :], -1), axis=1)
    slot_pick = slot_match.astype(bf16)
    arrived_ids = lax.all_to_all(
        slot_ids.reshape(land_count * dp_count, slot_count), everyone, split_axis=0, concat_axis=0, tiled=True
    )
    arrived_ids = arrived_ids.reshape(1, slot_total)

    mine, outgoing = [], None
    for h in range(parts):
        before = [outgoing] if h else []
        feat, outgoing = call(
            functools.partial(pick_body, land_count),
            [shape(group_rows, width, bf16), shape(slot_total, (h + 1) * width, bf16)],
            [keeps[h]] + sends[h] + before + [slot_pick],
            land,
            flops=2 * group_rows * slot_total * width,
        )
        mine.append(feat)
    arrived = lax.all_to_all(
        outgoing.reshape(land_count * dp_count, slot_count, keep_width),
        everyone,
        split_axis=0,
        concat_axis=0,
        tiled=True,
    )
    arrived = arrived.reshape(slot_total, keep_width)
    others = [land_send(mine[h], land_count - s) for s in range(1, land_count) for h in range(parts)]

    cent_block = centroids.shape[0]
    block = min(256, cent_block)

    def by_block(body, feats, more):
        tile = pl.BlockSpec((group_rows, block), lambda i: (0, i))
        return pl.pallas_call(
            functools.partial(body, land_count, parts),
            grid=(cent_block // block,),
            out_shape=shape(group_rows, cent_block, f32),
            in_specs=[SMEM]
            + [pl.BlockSpec((group_rows, width), lambda i: (0, 0))] * len(feats)
            + [pl.BlockSpec((block, feat_width), lambda i: (i, 0))]
            + [tile] * len(more),
            out_specs=tile,
            scratch_shapes=[pltpu.VMEM((group_rows, 1), f32)],
            cost_estimate=pl.CostEstimate(
                flops=2 * group_rows * cent_block * width * len(feats),
                bytes_accessed=2 * cent_block * feat_width + 4 * group_rows * cent_block * (1 + len(more)),
                transcendentals=0,
            ),
            compiler_params=pltpu.CompilerParams(vmem_limit_bytes=16 * 2**20),
        )(land, *feats, centroids, *more)

    near = by_block(near_body, mine, [])
    distances = by_block(distance_body, others, [near])
    (new_centroids,) = call(
        functools.partial(mean_body, land_count),
        [shape(own_width, feat_width, f32)],
        [arrived_ids, arrived],
        land,
        flops=2 * own_width * slot_total * keep_width,
    )
    return (distances, new_centroids)


def solution(mesh):
    return jax.shard_map(
        local,
        mesh=mesh,
        in_specs=(
            P(("dp", "land"), None),
            P(("land", "dp"), None),
            P(("land", "dp"), None),
            P("land", None),
            P("dp"),
        ),
        out_specs=(P("dp", "land"), P(("land", "dp"), None)),
        check_vma=False,
    )
```

```python
import functools

import jax
import jax.numpy as jnp
from jax import lax
from jax.experimental import pallas as pl
from jax.experimental.pallas import tpu as pltpu
from jax.sharding import PartitionSpec as P


EPSILON = 1e-06
SHARPNESS = 6.0
LANES = 128
VMEM = pl.BlockSpec(memory_space=pltpu.VMEM)
SMEM = pl.BlockSpec(memory_space=pltpu.SMEM)


def split_dp(count):
    cores = 2 if count % 2 == 0 else 1
    outer = 4 if (count // cores) % 4 == 0 else 1
    return outer, count // cores // outer, cores


def partner(index, size, step):
    return index ^ step if size & (size - 1) == 0 else (index + step) % size


def offset_of(target, own, size):
    return target ^ own if size & (size - 1) == 0 else (target - own + size) % size


def axis_perm(sizes, axis, step):
    outer, middle, cores = sizes
    pairs = []
    for z in range(outer):
        for y in range(middle):
            for c in range(cores):
                target = [z, y, c]
                target[axis] = partner(target[axis], sizes[axis], step)
                pairs.append(((z * middle + y) * cores + c, (target[0] * middle + target[1]) * cores + target[2]))
    return pairs


def call(body, outs, args, land, scratch=(), flops=0, limit=24):
    moved = sum(a.size * a.dtype.itemsize for a in list(args) + list(outs))
    return pl.pallas_call(
        body,
        out_shape=list(outs),
        in_specs=[SMEM] + [VMEM] * len(args),
        out_specs=[VMEM] * len(outs),
        scratch_shapes=[pltpu.VMEM(*s) for s in scratch],
        cost_estimate=pl.CostEstimate(flops=flops, bytes_accessed=moved, transcendentals=0),
        compiler_params=pltpu.CompilerParams(vmem_limit_bytes=limit * 2**20),
    )(land, *args)


def column_to_row(column):
    wide = jnp.broadcast_to(column, (column.shape[0], 128))
    return jnp.transpose(wide)[0:1]


def stage_body(land_ref, *refs):
    for src, out in zip(refs[: len(refs) // 2], refs[len(refs) // 2 :]):
        out[...] = src[...]


def kernel_body(land_count, cores, pieces, land_ref, *refs):
    count = land_count * cores
    row_refs, mark_refs = refs[:count], refs[count : count + pieces]
    out_ref, marks = refs[count + pieces :]
    depth, width = mark_refs[0].shape
    rows = row_refs[0].shape[0]
    for i, piece in enumerate(mark_refs):
        marks[i * depth : (i + 1) * depth] = piece[...]
    square = jnp.square(marks[...].astype(jnp.float32))
    mark_scale = column_to_row(lax.rsqrt(jnp.sum(square, axis=1, keepdims=True) / width + EPSILON))
    for g in range(cores):
        for s in range(land_count):
            source = lax.rem(land_ref[0] + s, land_count)
            values = row_refs[g * land_count + s][...]
            square = jnp.square(values.astype(jnp.float32))
            scale = lax.rsqrt(jnp.sum(square, axis=1, keepdims=True) / width + EPSILON) / width
            dots = lax.dot_general(values, marks[...], (((1,), (1,)), ((), ())), preferred_element_type=jnp.float32)
            similarity = dots * scale * mark_scale
            offset = pl.multiple_of(g * land_count * rows + source * rows, rows)
            out_ref[pl.ds(offset, rows), :] = jnp.exp(SHARPNESS * (similarity - 1.0)).astype(out_ref.dtype)


def partial_body(land_count, cores, pieces, start, land_ref, kern_ref, *refs):
    piece_refs, (own_ref, *others, block) = refs[:pieces], refs[pieces:]
    depth, full = piece_refs[0].shape
    keep_width = full // land_count
    width = block.shape[1]
    rows = own_ref.shape[0]
    for s in range(land_count):
        source = lax.rem(land_ref[0] + s, land_count)
        columns = pl.ds(pl.multiple_of(source * keep_width + start, LANES), width)
        for i, piece in enumerate(piece_refs):
            block[i * depth : (i + 1) * depth] = piece[:, columns]
        for g in reversed(range(cores)):
            out = own_ref if g == 0 else others[g - 1]
            value = jnp.dot(kern_ref[g * rows : (g + 1) * rows], block[...], preferred_element_type=jnp.float32)
            out[:, s * width : (s + 1) * width] = value.astype(out.dtype)


def add_body(count, land_ref, *refs):
    ins, outs = refs[:count], refs[count:]
    width = outs[0].shape[1]
    for s, out in enumerate(outs):
        total = ins[0][:, s * width : (s + 1) * width]
        for part in ins[1:]:
            total = total + part[:, s * width : (s + 1) * width].astype(jnp.float32)
        out[...] = total.astype(out.dtype)


def pick_body(count, tags, land_ref, *refs):
    ins, (pick_ref, *refs) = refs[:count], refs[count:]
    feat_ref, *outs = refs[tags:]
    total = ins[0][...].astype(jnp.float32)
    for part in ins[1:]:
        total = total + part[...].astype(jnp.float32)
    features = total.astype(feat_ref.dtype)
    feat_ref[...] = features
    width, rows = features.shape[1], outs[0].shape[0]
    for i, out in enumerate(outs):
        pick = pick_ref[i * rows : (i + 1) * rows]
        out[:, :width] = jnp.dot(pick, features, preferred_element_type=jnp.float32).astype(out.dtype)
        if tags:
            value = jnp.dot(pick, refs[0][...], preferred_element_type=jnp.float32)
            out[:, width:] = value.astype(out.dtype)


def take_body(plan, land_ref, *refs):
    *ins, out_ref = refs
    at = 0
    for i, start, rows in plan:
        out_ref[at : at + rows] = ins[i][start : start + rows]
        at += rows


def over_slots(match, values):
    return lax.dot_general(match, values, (((0,), (0,)), ((), ())), preferred_element_type=jnp.float32)


def peer_mean_body(plan, peers, slot_count, table_ref, *refs):
    ins, refs = refs[: 1 + max(i for i, _, _ in plan)], refs[1 + max(i for i, _, _ in plan) :]
    own_ref, *sends, match_ref, count_ref, arrived, matched = refs
    take_body(plan, table_ref, *ins, arrived)
    slots, own_width = matched.shape
    values = arrived[:, : own_ref.shape[1]]
    tags = arrived[:, own_ref.shape[1] :].astype(jnp.float32)
    lane = lax.broadcasted_iota(jnp.int32, (slots, own_width), 1).astype(jnp.float32)
    ones = jnp.ones((slots, own_width), jnp.bfloat16)
    for s, out in enumerate([own_ref, *sends]):
        match = (tags == lane + (1 + s * own_width)).astype(jnp.float32).astype(jnp.bfloat16)
        counts = over_slots(match, ones)
        out[...] = (over_slots(match, values) / jnp.maximum(counts, 1.0)).astype(out.dtype)
        if s == 0:
            matched[...] = match
            count_ref[...] = counts
    for d in range(peers):
        start = pl.multiple_of(table_ref[d], slot_count)
        match_ref[d * slot_count : (d + 1) * slot_count] = matched[pl.ds(start, slot_count), :]


def join_body(land_count, land_ref, match_ref, count_ref, arrived_ref, *refs):
    *means, out_ref = refs
    slots, width = match_ref.shape[0], arrived_ref.shape[1]
    first = means[0].shape[1]
    keep_width = first + width
    scale = jnp.maximum(count_ref[:, 0:1], 1.0)
    for j in range(land_count):
        sums = over_slots(match_ref[...], arrived_ref[j * slots : (j + 1) * slots])
        out_ref[:, j * keep_width + first : (j + 1) * keep_width] = sums / scale
    for s, mean in enumerate(means):
        source = lax.rem(land_ref[0] + land_count - s, land_count)
        columns = pl.ds(pl.multiple_of(source * keep_width, LANES), first)
        out_ref[:, columns] = mean[...].astype(jnp.float32)


def square_sum(parts):
    total = None
    for part in parts:
        term = jnp.sum(jnp.square(part[...].astype(jnp.float32)), axis=1, keepdims=True)
        total = term if total is None else total + term
    return total


def cross_sum(feats, cent_ref, first, land_count, parts, land_ref):
    keep_width = sum(feat.shape[1] for feat in feats[:parts])
    cross, at = None, 0
    for i, feat in enumerate(feats):
        at = 0 if i % parts == 0 else at
        source = lax.rem(land_ref[0] + first + i // parts, land_count)
        columns = pl.ds(pl.multiple_of(source * keep_width + at, LANES), feat.shape[1])
        at += feat.shape[1]
        term = lax.dot_general(
            feat[...], cent_ref[:, columns], (((1,), (1,)), ((), ())), preferred_element_type=jnp.float32
        )
        cross = term if cross is None else cross + term
    return cross


def near_body(land_count, parts, land_ref, *refs):
    *feats, cent_ref, out_ref, feat_sq = refs

    @pl.when(pl.program_id(0) == 0)
    def _():
        feat_sq[...] = square_sum(feats)

    cent_sq = column_to_row(jnp.sum(jnp.square(cent_ref[...].astype(jnp.float32)), axis=1, keepdims=True))
    cross = cross_sum(feats, cent_ref, 0, land_count, parts, land_ref)
    out_ref[...] = feat_sq[...] + cent_sq - 2.0 * cross


def distance_body(land_count, parts, land_ref, *refs):
    *feats, cent_ref, near_ref, out_ref, feat_sq = refs

    @pl.when(pl.program_id(0) == 0)
    def _():
        feat_sq[...] = square_sum(feats)

    cross = cross_sum(feats, cent_ref, 1, land_count, parts, land_ref)
    out_ref[...] = (near_ref[...] + feat_sq[...] - 2.0 * cross) / cent_ref.shape[1]


def mean_body(land_count, land_ref, ids_ref, arrived_ref, out_ref):
    own_width, width = out_ref.shape[0], arrived_ref.shape[1]
    slots = ids_ref.shape[1] // land_count
    for j in range(land_count):
        match = ids_ref[:, j * slots : (j + 1) * slots] == lax.broadcasted_iota(jnp.int32, (own_width, slots), 0)
        match = match.astype(jnp.float32)
        counts = jnp.sum(match, axis=1, keepdims=True)
        part = arrived_ref[j * slots : (j + 1) * slots]
        sums = jnp.dot(match.astype(jnp.bfloat16), part, preferred_element_type=jnp.float32)
        out_ref[:, j * width : (j + 1) * width] = sums / jnp.maximum(counts, 1.0)


def column_parts(feat_width, land_count, own_width):
    keep_width = feat_width // land_count
    if keep_width > LANES and own_width == LANES and land_count * own_width <= 256:
        return [LANES, keep_width - LANES]
    return [keep_width]


def local(embeddings, landmarks, factor, centroids, assignment):
    land_count = lax.axis_size("land")
    dp_count = lax.axis_size("dp")
    land_id = lax.axis_index("land")
    land = land_id.astype(jnp.int32).reshape(1)
    sizes = split_dp(dp_count)
    cores = sizes[2]
    own_rows, embed_width = embeddings.shape
    feat_width = factor.shape[1]
    group_rows = own_rows * land_count
    bf16, f32 = jnp.bfloat16, jnp.float32

    def shape(rows, columns, dtype):
        return jax.ShapeDtypeStruct((rows, columns), dtype)

    def move(x, axis, step):
        return lax.ppermute(x, "dp", axis_perm(sizes, axis, step))

    def land_send(x, step):
        return lax.ppermute(x, "land", [(s, (s + step) % land_count) for s in range(land_count)])

    def along_z(x):
        pieces = [x]
        for k in range(1, sizes[0]):
            relayed = sizes[0] == 4 and k == 3
            pieces.append(move(pieces[2] if relayed else x, 0, 1 if relayed else k))
        return pieces

    def along_y(pieces, relay):
        out = list(pieces)
        for k in range(1, sizes[1]):
            first = move(pieces[0], 1, k)
            for i, piece in enumerate(pieces):
                if i == 0:
                    out.append(first)
                elif i == 1 and relay:
                    out.append(move(first, 0, 1))
                else:
                    out.append(move(piece, 1, k))
        return out

    row_pieces = [embeddings] + [land_send(embeddings, land_count - k) for k in range(1, land_count)]
    row_pieces = row_pieces + [move(p, 2, k) for k in range(1, cores) for p in row_pieces]
    marks = along_y(along_z(landmarks), False)
    own_width = centroids.shape[0] // dp_count
    widths = column_parts(feat_width, land_count, own_width)
    parts = len(widths)
    factors = along_y(along_z(factor), sizes[0] > 1)

    rows_all = group_rows * cores
    depth_all = landmarks.shape[0] * len(marks)
    row_pieces[0], marks[0], factors[0] = call(
        stage_body,
        [shape(*a.shape, a.dtype) for a in (embeddings, landmarks, factor)],
        [embeddings, landmarks, factor],
        land,
    )
    (kern,) = call(
        functools.partial(kernel_body, land_count, cores, len(marks)),
        [shape(rows_all, depth_all, bf16)],
        row_pieces + marks,
        land,
        scratch=[((depth_all, embed_width), bf16)],
        flops=2 * rows_all * depth_all * embed_width,
    )
    keeps, sends = [], []
    for h, width in enumerate(widths):
        own, *others = call(
            functools.partial(partial_body, land_count, cores, len(factors), sum(widths[:h])),
            [shape(group_rows, land_count * width, f32)]
            + [shape(group_rows, land_count * width, bf16)] * (cores - 1),
            [kern] + factors,
            land,
            scratch=[((depth_all, width), bf16)],
            flops=2 * rows_all * depth_all * land_count * width,
        )
        others = [move(o, 2, cores - g) for g, o in enumerate(others, 1)]
        keep, *send = call(
            functools.partial(add_body, cores), [shape(group_rows, width, bf16)] * land_count, [own] + others, land
        )
        keeps.append(keep)
        sends.append([land_send(x, s) for s, x in enumerate(send, 1)])

    assignment, dp_id, land_late, _ = lax.optimization_barrier(
        (assignment, lax.axis_index("dp"), land_id, keeps[0])
    )
    slot_count = 2 * max(1, group_rows // (land_count * dp_count))
    peer_slots = land_count * slot_count
    slot_total = dp_count * peer_slots
    slice_id = assignment // own_width
    local_id = assignment % own_width
    row_pos = lax.iota(jnp.int32, group_rows)
    earlier = (slice_id[None, :] == slice_id[:, None]) & (row_pos[None, :] < row_pos[:, None])
    slot_rank = jnp.sum(earlier.astype(jnp.int32), axis=1)
    slot_pos = lax.iota(jnp.int32, slot_total)[:, None]
    owner_match = slot_pos == (slice_id * slot_count + slot_rank)[None, :]
    everyone = ("land", "dp")

    def pick(h, blocks, rows, one_hot, tags):
        feat, *picked = call(
            functools.partial(pick_body, land_count, len(tags)),
            [shape(group_rows, widths[h], bf16)]
            + [shape(rows, widths[h] + sum(t.shape[1] for t in tags), bf16)] * blocks,
            [keeps[h]] + sends[h] + [one_hot.astype(bf16)] + tags,
            land,
            flops=2 * group_rows * blocks * rows * widths[h],
        )
        mine.append(feat)
        return picked

    mine, means = [], []
    if parts > 1:
        outer, middle, _ = sizes

        def places(index):
            return index // (middle * cores), index // cores % middle, index % cores

        target_dp = slice_id % dp_count
        land_offset = lax.rem(slice_id // dp_count - land_late + land_count, land_count)
        here = places(dp_id)
        away = [offset_of(t, o, n) for t, o, n in zip(places(target_dp), here, sizes)]
        block_of = (away[0] * middle + away[1]) * cores + away[2]
        peer_match = slot_pos == (block_of * peer_slots + land_offset * slot_count + slot_rank)[None, :]
        tag = (land_offset * own_width + local_id + 1).astype(f32).astype(bf16)
        tags = jnp.broadcast_to(tag[:, None], (group_rows, own_width))
        order = lax.iota(jnp.int32, dp_count)
        near = [offset_of(o, d, n) for o, d, n in zip(here, places(order), sizes)]
        table = ((near[2] * middle + near[1]) * outer + near[0]) * peer_slots
        held = pick(0, outer, middle * cores * peer_slots, peer_match, [tags])
        held = [held[0]] + [move(held[k], 0, k) for k in range(1, outer)]
        tagged = widths[0] + own_width

        def take(plan, ins):
            rows = sum(n for _, _, n in plan)
            return call(functools.partial(take_body, plan), [shape(rows, tagged, bf16)], ins, land)[0]

        plan = [(i, 0, cores * peer_slots) for i in range(outer)]
        for k in range(1, middle):
            line = [(i, k * cores * peer_slots, cores * peer_slots) for i in range(outer)]
            held.append(move(take(line, held[:outer]), 1, k))
            plan += [(len(held) - 1, i * cores * peer_slots, cores * peer_slots) for i in range(outer)]
        own_plan = [(i, start, peer_slots) for i, start, _ in plan]
        along = len(held)
        for k in range(1, cores):
            line = [(i, start + k * peer_slots, peer_slots) for i, start, _ in plan]
            held.append(move(take(line, held[:along]), 2, k))
            own_plan.append((len(held) - 1, 0, len(plan) * peer_slots))
        mean, *results = call(
            functools.partial(peer_mean_body, own_plan, dp_count, slot_count),
            [shape(own_width, widths[0], f32)]
            + [shape(own_width, widths[0], bf16)] * (land_count - 1)
            + [shape(dp_count * slot_count, own_width, bf16), shape(own_width, own_width, f32)],
            held,
            table,
            scratch=[((slot_total, tagged), bf16), ((slot_total, own_width), bf16)],
            flops=4 * land_count * own_width * slot_total * widths[0],
        )
        *far, slot_owner, counts = results
        means = [mean] + [land_send(m, s) for s, m in enumerate(far, 1)]
    else:
        slot_ids = jnp.max(jnp.where(owner_match, local_id[None, :], -1), axis=1)
        arrived_ids = lax.all_to_all(
            slot_ids.reshape(land_count * dp_count, slot_count), everyone, split_axis=0, concat_axis=0, tiled=True
        )
        arrived_ids = arrived_ids.reshape(1, slot_total)
    (outgoing,) = pick(parts - 1, 1, slot_total, owner_match, [])
    arrived = lax.all_to_all(
        outgoing.reshape(land_count * dp_count, slot_count, widths[-1]),
        everyone,
        split_axis=0,
        concat_axis=0,
        tiled=True,
    )
    arrived = arrived.reshape(slot_total, widths[-1])
    others = [land_send(mine[h], land_count - s) for s in range(1, land_count) for h in range(parts)]

    cent_block = centroids.shape[0]
    block = min(256, cent_block)

    def by_block(body, feats, more):
        tile = pl.BlockSpec((group_rows, block), lambda i: (0, i))
        return pl.pallas_call(
            functools.partial(body, land_count, parts),
            grid=(cent_block // block,),
            out_shape=shape(group_rows, cent_block, f32),
            in_specs=[SMEM]
            + [pl.BlockSpec(f.shape, lambda i: (0, 0)) for f in feats]
            + [pl.BlockSpec((block, feat_width), lambda i: (i, 0))]
            + [tile] * len(more),
            out_specs=tile,
            scratch_shapes=[pltpu.VMEM((group_rows, 1), f32)],
            cost_estimate=pl.CostEstimate(
                flops=2 * group_rows * cent_block * sum(f.shape[1] for f in feats),
                bytes_accessed=2 * cent_block * feat_width + 4 * group_rows * cent_block * (1 + len(more)),
                transcendentals=0,
            ),
            compiler_params=pltpu.CompilerParams(vmem_limit_bytes=16 * 2**20),
        )(land, *feats, centroids, *more)

    near = by_block(near_body, mine, [])
    distances = by_block(distance_body, others, [near])
    if parts > 1:
        body, ins = functools.partial(join_body, land_count), [slot_owner, counts, arrived] + means
    else:
        body, ins = functools.partial(mean_body, land_count), [arrived_ids, arrived]
    (new_centroids,) = call(
        body, [shape(own_width, feat_width, f32)], ins, land, flops=2 * own_width * slot_total * widths[-1]
    )
    return (distances, new_centroids)


def solution(mesh):
    return jax.shard_map(
        local,
        mesh=mesh,
        in_specs=(
            P(("dp", "land"), None),
            P(("land", "dp"), None),
            P(("land", "dp"), None),
            P("land", None),
            P("dp"),
        ),
        out_specs=(P("dp", "land"), P(("land", "dp"), None)),
        check_vma=False,
    )
```

```python
import functools

import jax
import jax.numpy as jnp
from jax import lax
from jax.experimental import pallas as pl
from jax.experimental.pallas import tpu as pltpu
from jax.sharding import PartitionSpec as P


EPSILON = 1e-06
SHARPNESS = 6.0
LANES = 128
VMEM = pl.BlockSpec(memory_space=pltpu.VMEM)
SMEM = pl.BlockSpec(memory_space=pltpu.SMEM)


def split_dp(count):
    cores = 2 if count % 2 == 0 else 1
    outer = 4 if (count // cores) % 4 == 0 else 1
    return outer, count // cores // outer, cores


def partner(index, size, step):
    return index ^ step if size & (size - 1) == 0 else (index + step) % size


def offset_of(target, own, size):
    return target ^ own if size & (size - 1) == 0 else (target - own + size) % size


def axis_perm(sizes, axis, step):
    outer, middle, cores = sizes
    pairs = []
    for z in range(outer):
        for y in range(middle):
            for c in range(cores):
                target = [z, y, c]
                target[axis] = partner(target[axis], sizes[axis], step)
                pairs.append(((z * middle + y) * cores + c, (target[0] * middle + target[1]) * cores + target[2]))
    return pairs


def call(body, outs, args, land, scratch=(), flops=0, limit=24):
    moved = sum(a.size * a.dtype.itemsize for a in list(args) + list(outs))
    return pl.pallas_call(
        body,
        out_shape=list(outs),
        in_specs=[SMEM] + [VMEM] * len(args),
        out_specs=[VMEM] * len(outs),
        scratch_shapes=[pltpu.VMEM(*s) for s in scratch],
        cost_estimate=pl.CostEstimate(flops=flops, bytes_accessed=moved, transcendentals=0),
        compiler_params=pltpu.CompilerParams(vmem_limit_bytes=limit * 2**20),
    )(land, *args)


def column_to_row(column):
    wide = jnp.broadcast_to(column, (column.shape[0], 128))
    return jnp.transpose(wide)[0:1]


def stage_body(land_ref, *refs):
    for src, out in zip(refs[: len(refs) // 2], refs[len(refs) // 2 :]):
        out[...] = src[...]


def kernel_body(land_count, cores, pieces, land_ref, *refs):
    count = land_count * cores
    row_refs, mark_refs = refs[:count], refs[count : count + pieces]
    out_ref, marks = refs[count + pieces :]
    depth, width = mark_refs[0].shape
    rows = row_refs[0].shape[0]
    for i, piece in enumerate(mark_refs):
        marks[i * depth : (i + 1) * depth] = piece[...]
    square = jnp.square(marks[...].astype(jnp.float32))
    mark_scale = column_to_row(lax.rsqrt(jnp.sum(square, axis=1, keepdims=True) / width + EPSILON))
    for g in range(cores):
        for s in range(land_count):
            source = lax.rem(land_ref[0] + s, land_count)
            values = row_refs[g * land_count + s][...]
            square = jnp.square(values.astype(jnp.float32))
            scale = lax.rsqrt(jnp.sum(square, axis=1, keepdims=True) / width + EPSILON) / width
            dots = lax.dot_general(values, marks[...], (((1,), (1,)), ((), ())), preferred_element_type=jnp.float32)
            similarity = dots * scale * mark_scale
            offset = pl.multiple_of(g * land_count * rows + source * rows, rows)
            out_ref[pl.ds(offset, rows), :] = jnp.exp(SHARPNESS * (similarity - 1.0)).astype(out_ref.dtype)


def partial_body(land_count, cores, pieces, start, land_ref, kern_ref, *refs):
    piece_refs, (own_ref, *others, block) = refs[:pieces], refs[pieces:]
    depth, full = piece_refs[0].shape
    keep_width = full // land_count
    width = block.shape[1]
    rows = own_ref.shape[0]
    for s in range(land_count):
        source = lax.rem(land_ref[0] + s, land_count)
        columns = pl.ds(pl.multiple_of(source * keep_width + start, LANES), width)
        for i, piece in enumerate(piece_refs):
            block[i * depth : (i + 1) * depth] = piece[:, columns]
        for g in reversed(range(cores)):
            out = own_ref if g == 0 else others[g - 1]
            value = jnp.dot(kern_ref[g * rows : (g + 1) * rows], block[...], preferred_element_type=jnp.float32)
            out[:, s * width : (s + 1) * width] = value.astype(out.dtype)


def add_body(count, land_ref, *refs):
    ins, outs = refs[:count], refs[count:]
    width = outs[0].shape[1]
    for s, out in enumerate(outs):
        total = ins[0][:, s * width : (s + 1) * width]
        for part in ins[1:]:
            total = total + part[:, s * width : (s + 1) * width].astype(jnp.float32)
        out[...] = total.astype(out.dtype)


def pick_body(count, tags, land_ref, *refs):
    ins, (pick_ref, *refs) = refs[:count], refs[count:]
    feat_ref, *outs = refs[tags:]
    total = ins[0][...].astype(jnp.float32)
    for part in ins[1:]:
        total = total + part[...].astype(jnp.float32)
    features = total.astype(feat_ref.dtype)
    feat_ref[...] = features
    width, rows = features.shape[1], outs[0].shape[0]
    for i, out in enumerate(outs):
        pick = pick_ref[i * rows : (i + 1) * rows]
        out[:, :width] = jnp.dot(pick, features, preferred_element_type=jnp.float32).astype(out.dtype)
        if tags:
            value = jnp.dot(pick, refs[0][...], preferred_element_type=jnp.float32)
            out[:, width:] = value.astype(out.dtype)


def take_body(plan, land_ref, *refs):
    *ins, out_ref = refs
    at = 0
    for i, start, rows in plan:
        out_ref[at : at + rows] = ins[i][start : start + rows]
        at += rows


def over_slots(match, values):
    return lax.dot_general(match, values, (((0,), (0,)), ((), ())), preferred_element_type=jnp.float32)


def peer_mean_body(plan, peers, slot_count, table_ref, *refs):
    ins, refs = refs[: 1 + max(i for i, _, _ in plan)], refs[1 + max(i for i, _, _ in plan) :]
    own_ref, *sends, match_ref, count_ref, arrived, matched = refs
    take_body(plan, table_ref, *ins, arrived)
    slots, own_width = matched.shape
    width = own_ref.shape[1]
    tags = arrived[:, width:].astype(jnp.float32)
    lane = lax.broadcasted_iota(jnp.int32, (slots, own_width), 1).astype(jnp.float32)
    arrived[:, width:] = jnp.ones((slots, own_width), jnp.bfloat16)
    values = arrived[...]
    for s, out in enumerate([own_ref, *sends]):
        match = (tags == lane + (1 + s * own_width)).astype(jnp.float32).astype(jnp.bfloat16)
        sums = over_slots(match, values)
        counts = sums[:, width:]
        out[...] = (sums[:, :width] / jnp.maximum(counts, 1.0)).astype(out.dtype)
        if s == 0:
            matched[...] = match
            count_ref[...] = counts
    for d in range(peers):
        start = pl.multiple_of(table_ref[d], slot_count)
        match_ref[d * slot_count : (d + 1) * slot_count] = matched[pl.ds(start, slot_count), :]


def join_body(land_count, land_ref, match_ref, count_ref, arrived_ref, *refs):
    *means, out_ref = refs
    slots, width = match_ref.shape[0], arrived_ref.shape[1]
    first = means[0].shape[1]
    keep_width = first + width
    scale = jnp.maximum(count_ref[:, 0:1], 1.0)
    for j in range(land_count):
        sums = over_slots(match_ref[...], arrived_ref[j * slots : (j + 1) * slots])
        out_ref[:, j * keep_width + first : (j + 1) * keep_width] = sums / scale
    for s, mean in enumerate(means):
        source = lax.rem(land_ref[0] + land_count - s, land_count)
        columns = pl.ds(pl.multiple_of(source * keep_width, LANES), first)
        out_ref[:, columns] = mean[...].astype(jnp.float32)


def square_sum(parts):
    total = None
    for part in parts:
        term = jnp.sum(jnp.square(part[...].astype(jnp.float32)), axis=1, keepdims=True)
        total = term if total is None else total + term
    return total


def cross_sum(feats, cent_ref, first, land_count, parts, land_ref):
    keep_width = sum(feat.shape[1] for feat in feats[:parts])
    cross, at = None, 0
    for i, feat in enumerate(feats):
        at = 0 if i % parts == 0 else at
        source = lax.rem(land_ref[0] + first + i // parts, land_count)
        columns = pl.ds(pl.multiple_of(source * keep_width + at, LANES), feat.shape[1])
        at += feat.shape[1]
        term = lax.dot_general(
            feat[...], cent_ref[:, columns], (((1,), (1,)), ((), ())), preferred_element_type=jnp.float32
        )
        cross = term if cross is None else cross + term
    return cross


def near_body(land_count, parts, land_ref, *refs):
    *feats, cent_ref, out_ref, feat_sq = refs

    @pl.when(pl.program_id(0) == 0)
    def _():
        feat_sq[...] = square_sum(feats)

    cent_sq = column_to_row(jnp.sum(jnp.square(cent_ref[...].astype(jnp.float32)), axis=1, keepdims=True))
    cross = cross_sum(feats, cent_ref, 0, land_count, parts, land_ref)
    out_ref[...] = feat_sq[...] + cent_sq - 2.0 * cross


def distance_body(land_count, parts, land_ref, *refs):
    *feats, cent_ref, near_ref, out_ref, feat_sq = refs

    @pl.when(pl.program_id(0) == 0)
    def _():
        feat_sq[...] = square_sum(feats)

    cross = cross_sum(feats, cent_ref, 1, land_count, parts, land_ref)
    out_ref[...] = (near_ref[...] + feat_sq[...] - 2.0 * cross) / cent_ref.shape[1]


def mean_body(land_count, land_ref, ids_ref, arrived_ref, out_ref):
    own_width, width = out_ref.shape[0], arrived_ref.shape[1]
    slots = ids_ref.shape[1] // land_count
    for j in range(land_count):
        match = ids_ref[:, j * slots : (j + 1) * slots] == lax.broadcasted_iota(jnp.int32, (own_width, slots), 0)
        match = match.astype(jnp.float32)
        counts = jnp.sum(match, axis=1, keepdims=True)
        part = arrived_ref[j * slots : (j + 1) * slots]
        sums = jnp.dot(match.astype(jnp.bfloat16), part, preferred_element_type=jnp.float32)
        out_ref[:, j * width : (j + 1) * width] = sums / jnp.maximum(counts, 1.0)


def column_parts(feat_width, land_count, own_width):
    keep_width = feat_width // land_count
    if keep_width > LANES and own_width == LANES and land_count * own_width <= 256:
        return [LANES, keep_width - LANES]
    return [keep_width]


def local(embeddings, landmarks, factor, centroids, assignment):
    land_count = lax.axis_size("land")
    dp_count = lax.axis_size("dp")
    land_id = lax.axis_index("land")
    land = land_id.astype(jnp.int32).reshape(1)
    sizes = split_dp(dp_count)
    cores = sizes[2]
    own_rows, embed_width = embeddings.shape
    feat_width = factor.shape[1]
    group_rows = own_rows * land_count
    bf16, f32 = jnp.bfloat16, jnp.float32

    def shape(rows, columns, dtype):
        return jax.ShapeDtypeStruct((rows, columns), dtype)

    def move(x, axis, step):
        return lax.ppermute(x, "dp", axis_perm(sizes, axis, step))

    def land_send(x, step):
        return lax.ppermute(x, "land", [(s, (s + step) % land_count) for s in range(land_count)])

    def along_z(x):
        pieces = [x]
        for k in range(1, sizes[0]):
            relayed = sizes[0] == 4 and k == 3
            pieces.append(move(pieces[2] if relayed else x, 0, 1 if relayed else k))
        return pieces

    def along_y(pieces, relay):
        out = list(pieces)
        for k in range(1, sizes[1]):
            first = move(pieces[0], 1, k)
            for i, piece in enumerate(pieces):
                if i == 0:
                    out.append(first)
                elif i == 1 and relay:
                    out.append(move(first, 0, 1))
                else:
                    out.append(move(piece, 1, k))
        return out

    row_pieces = [embeddings] + [land_send(embeddings, land_count - k) for k in range(1, land_count)]
    row_pieces = row_pieces + [move(p, 2, k) for k in range(1, cores) for p in row_pieces]
    marks = along_y(along_z(landmarks), False)
    own_width = centroids.shape[0] // dp_count
    widths = column_parts(feat_width, land_count, own_width)
    parts = len(widths)
    factors = along_y(along_z(factor), sizes[0] > 1)

    rows_all = group_rows * cores
    depth_all = landmarks.shape[0] * len(marks)
    row_pieces[0], marks[0], factors[0] = call(
        stage_body,
        [shape(*a.shape, a.dtype) for a in (embeddings, landmarks, factor)],
        [embeddings, landmarks, factor],
        land,
    )
    (kern,) = call(
        functools.partial(kernel_body, land_count, cores, len(marks)),
        [shape(rows_all, depth_all, bf16)],
        row_pieces + marks,
        land,
        scratch=[((depth_all, embed_width), bf16)],
        flops=2 * rows_all * depth_all * embed_width,
    )
    keeps, sends = [], []
    for h, width in enumerate(widths):
        own, *others = call(
            functools.partial(partial_body, land_count, cores, len(factors), sum(widths[:h])),
            [shape(group_rows, land_count * width, f32)]
            + [shape(group_rows, land_count * width, bf16)] * (cores - 1),
            [kern] + factors,
            land,
            scratch=[((depth_all, width), bf16)],
            flops=2 * rows_all * depth_all * land_count * width,
        )
        others = [move(o, 2, cores - g) for g, o in enumerate(others, 1)]
        keep, *send = call(
            functools.partial(add_body, cores), [shape(group_rows, width, bf16)] * land_count, [own] + others, land
        )
        keeps.append(keep)
        sends.append([land_send(x, s) for s, x in enumerate(send, 1)])

    assignment, dp_id, land_late, _ = lax.optimization_barrier(
        (assignment, lax.axis_index("dp"), land_id, keeps[0])
    )
    slot_count = 2 * max(1, group_rows // (land_count * dp_count))
    peer_slots = land_count * slot_count
    slot_total = dp_count * peer_slots
    slice_id = assignment // own_width
    local_id = assignment % own_width
    row_pos = lax.iota(jnp.int32, group_rows)
    earlier = (slice_id[None, :] == slice_id[:, None]) & (row_pos[None, :] < row_pos[:, None])
    slot_rank = jnp.sum(earlier.astype(jnp.int32), axis=1)
    slot_pos = lax.iota(jnp.int32, slot_total)[:, None]
    owner_match = slot_pos == (slice_id * slot_count + slot_rank)[None, :]
    everyone = ("land", "dp")

    def pick(h, blocks, rows, one_hot, tags):
        feat, *picked = call(
            functools.partial(pick_body, land_count, len(tags)),
            [shape(group_rows, widths[h], bf16)]
            + [shape(rows, widths[h] + sum(t.shape[1] for t in tags), bf16)] * blocks,
            [keeps[h]] + sends[h] + [one_hot.astype(bf16)] + tags,
            land,
            flops=2 * group_rows * blocks * rows * widths[h],
        )
        mine.append(feat)
        return picked

    mine, means = [], []
    if parts > 1:
        outer, middle, _ = sizes

        def places(index):
            return index // (middle * cores), index // cores % middle, index % cores

        target_dp = slice_id % dp_count
        land_offset = lax.rem(slice_id // dp_count - land_late + land_count, land_count)
        here = places(dp_id)
        away = [offset_of(t, o, n) for t, o, n in zip(places(target_dp), here, sizes)]
        block_of = (away[0] * middle + away[1]) * cores + away[2]
        peer_match = slot_pos == (block_of * peer_slots + land_offset * slot_count + slot_rank)[None, :]
        tag = (land_offset * own_width + local_id + 1).astype(f32).astype(bf16)
        tags = jnp.broadcast_to(tag[:, None], (group_rows, own_width))
        order = lax.iota(jnp.int32, dp_count)
        near = [offset_of(o, d, n) for o, d, n in zip(here, places(order), sizes)]
        table = ((near[2] * middle + near[1]) * outer + near[0]) * peer_slots
        held = pick(0, outer, middle * cores * peer_slots, peer_match, [tags])
        held = [held[0]] + [move(held[k], 0, k) for k in range(1, outer)]
        tagged = widths[0] + own_width

        def take(plan, ins):
            rows = sum(n for _, _, n in plan)
            return call(functools.partial(take_body, plan), [shape(rows, tagged, bf16)], ins, land)[0]

        plan = [(i, 0, cores * peer_slots) for i in range(outer)]
        for k in range(1, middle):
            line = [(i, k * cores * peer_slots, cores * peer_slots) for i in range(outer)]
            held.append(move(take(line, held[:outer]), 1, k))
            plan += [(len(held) - 1, i * cores * peer_slots, cores * peer_slots) for i in range(outer)]
        own_plan = [(i, start, peer_slots) for i, start, _ in plan]
        along = len(held)
        for k in range(1, cores):
            line = [(i, start + k * peer_slots, peer_slots) for i, start, _ in plan]
            held.append(move(take(line, held[:along]), 2, k))
            own_plan.append((len(held) - 1, 0, len(plan) * peer_slots))
        mean, *results = call(
            functools.partial(peer_mean_body, own_plan, dp_count, slot_count),
            [shape(own_width, widths[0], f32)]
            + [shape(own_width, widths[0], bf16)] * (land_count - 1)
            + [shape(dp_count * slot_count, own_width, bf16), shape(own_width, own_width, f32)],
            held,
            table,
            scratch=[((slot_total, tagged), bf16), ((slot_total, own_width), bf16)],
            flops=4 * land_count * own_width * slot_total * widths[0],
        )
        *far, slot_owner, counts = results
        means = [mean] + [land_send(m, s) for s, m in enumerate(far, 1)]
    else:
        slot_ids = jnp.max(jnp.where(owner_match, local_id[None, :], -1), axis=1)
        arrived_ids = lax.all_to_all(
            slot_ids.reshape(land_count * dp_count, slot_count), everyone, split_axis=0, concat_axis=0, tiled=True
        )
        arrived_ids = arrived_ids.reshape(1, slot_total)
    (outgoing,) = pick(parts - 1, 1, slot_total, owner_match, [])
    arrived = lax.all_to_all(
        outgoing.reshape(land_count * dp_count, slot_count, widths[-1]),
        everyone,
        split_axis=0,
        concat_axis=0,
        tiled=True,
    )
    arrived = arrived.reshape(slot_total, widths[-1])
    others = [land_send(mine[h], land_count - s) for s in range(1, land_count) for h in range(parts)]

    cent_block = centroids.shape[0]
    block = min(256, cent_block)

    def by_block(body, feats, more):
        tile = pl.BlockSpec((group_rows, block), lambda i: (0, i))
        return pl.pallas_call(
            functools.partial(body, land_count, parts),
            grid=(cent_block // block,),
            out_shape=shape(group_rows, cent_block, f32),
            in_specs=[SMEM]
            + [pl.BlockSpec(f.shape, lambda i: (0, 0)) for f in feats]
            + [pl.BlockSpec((block, feat_width), lambda i: (i, 0))]
            + [tile] * len(more),
            out_specs=tile,
            scratch_shapes=[pltpu.VMEM((group_rows, 1), f32)],
            cost_estimate=pl.CostEstimate(
                flops=2 * group_rows * cent_block * sum(f.shape[1] for f in feats),
                bytes_accessed=2 * cent_block * feat_width + 4 * group_rows * cent_block * (1 + len(more)),
                transcendentals=0,
            ),
            compiler_params=pltpu.CompilerParams(vmem_limit_bytes=16 * 2**20),
        )(land, *feats, centroids, *more)

    near = by_block(near_body, mine, [])
    distances = by_block(distance_body, others, [near])
    if parts > 1:
        body, ins = functools.partial(join_body, land_count), [slot_owner, counts, arrived] + means
    else:
        body, ins = functools.partial(mean_body, land_count), [arrived_ids, arrived]
    (new_centroids,) = call(
        body, [shape(own_width, feat_width, f32)], ins, land, flops=2 * own_width * slot_total * widths[-1]
    )
    return (distances, new_centroids)


def solution(mesh):
    return jax.shard_map(
        local,
        mesh=mesh,
        in_specs=(
            P(("dp", "land"), None),
            P(("land", "dp"), None),
            P(("land", "dp"), None),
            P("land", None),
            P("dp"),
        ),
        out_specs=(P("dp", "land"), P(("land", "dp"), None)),
        check_vma=False,
    )
```
